1024 devices in a mesh: pipe: 8 (over y_hi, x), expert: 32 (over z, core), dp: 4 (over y_lo).
Axes of the slice: x: 4, y: 8 (y_hi: 2, y_lo: 4; y = y_hi * 4 + y_lo), z: 16, core: 2. Of those that a mesh axis runs over, the one named last changes fastest.
Arguments:
- acts_fwd: bfloat16 [8, 512, 3584], P('pipe', ('expert', 'dp')), may hold values from -6 to 6
- ids_fwd: int32 [8, 512, 2], P('pipe', ('expert', 'dp')), may hold values from 0 to 3, all different within a row; in each aligned block of 4 rows (0 to 3, 4 to 7, ..., all dimensions but the last counted through in order) at most 3 rows name the same one
- scores_fwd: float32 [8, 512, 2], P('pipe', ('expert', 'dp')), may hold values from 0.05 to 0.95
- cot_bwd: bfloat16 [8, 512, 3584], P('pipe', ('expert', 'dp')), may hold values from -1.5 to 1.5
- ids_bwd: int32 [8, 512, 2], P('pipe', ('expert', 'dp')), may hold values from 0 to 3, all different within a row; in each aligned block of 4 rows (0 to 3, 4 to 7, ..., all dimensions but the last counted through in order) at most 3 rows name the same one
- scores_bwd: float32 [8, 512, 2], P('pipe', ('expert', 'dp')), may hold values from 0.05 to 0.95
- saved_out: bfloat16 [8, 512, 2, 3584], P('pipe', ('expert', 'dp')), may hold values from -1.5 to 1.5
- saved_pre: bfloat16 [8, 384, 2, 8192], P('pipe', 'dp', None, 'expert'), may hold values from -6 to 6
- w_gate: bfloat16 [8, 3584, 8192], P('pipe', None, 'expert'), may hold values from -0.09375 to 0.09375
- w_up: bfloat16 [8, 3584, 8192], P('pipe', None, 'expert'), may hold values from -0.09375 to 0.09375
- w_down: bfloat16 [8, 8192, 3584], P('pipe', 'expert'), may hold values from -0.125 to 0.125
Outputs:
- acts_sent: bfloat16 [8, 512, 3584], P('pipe', ('expert', 'dp'))
- grads_sent: bfloat16 [8, 512, 3584], P('pipe', ('expert', 'dp'))
- score_grads: float32 [8, 512, 2], P('pipe', ('expert', 'dp'))
- down_grad: float32 [8, 3584, 8192], P('pipe', 'dp', 'expert')
The draws below stay inside these ranges and needn't reach their ends.
Inputs may be any that keep to these rules, and one draw needn't show every extreme that they name: `ids_fwd`: each row names 2 different experts. In the 4 rows of one device no expert is named more than 3 times, and in every draw some device names one expert exactly 3 times. `ids_bwd`: each row names 2 different experts. In the 4 rows of one device no expert is named more than 3 times, and in every draw some device names one expert exactly 3 times.
All inputs are finite; a program needn't handle non-finite values.
Results may differ from the reference program's by a relative error of at most 0.0059.
Values may be sent and summed in bfloat16 or wider, within the bound.
A program may use at most 32 MiB of HBM per device.

```python
import math
import jax
import jax.numpy as jnp
import numpy as np
from jax import lax

D = 3584
FE = 2048
TOK_DEV = 4
SECTIONS = 8
EXPERTS = 4
TOP = 2
CAP = 3
TOKENS = 512
ROWS = 384
N_EXPERT = 32
N_DP = 4


def shard_levels(own_key, shape, shards, least, largest):
    def one(dim, shards_of):
        draws = jax.random.uniform(jax.random.fold_in(jax.random.fold_in(own_key, 6), dim), (shards_of,), jnp.float32, least / len(shards), largest / len(shards))
        return jnp.repeat(jnp.exp(draws), shape[dim] // shards_of).reshape((-1,) + (1,) * (len(shape) - dim - 1))

    level = one(*shards[0])
    for cut in shards[1:]:
        level = level * one(*cut)
    return level


def routed_block(key, own, number, rows, number_of, top, most, slope):
    ranking = jax.random.permutation(key, number_of)
    crowded, usual = load_shares(number_of, rows * top, most, slope, True), load_shares(number_of, rows * top, most, slope, False)
    places = jnp.arange(number_of)

    def named(sizes, offset_by):
        used = int((sizes > 0).sum())
        fixed = max(1, used // 4)
        passed = fixed + (places - fixed + offset_by * (used - fixed)) % max(1, number_of - fixed)
        return jnp.zeros((number_of,), jnp.int32).at[ranking[jnp.where(places < fixed, places, passed)]].set(jnp.asarray(sizes, jnp.int32))

    sizes = jnp.where(number % 4 == 0, named(crowded, number // 4), named(usual, number - number // 4 - 1))
    mixed = jax.random.permutation(jax.random.fold_in(own, 3), number_of)
    donor, sink = mixed[0:number_of // 2 * 2:2], mixed[1:number_of // 2 * 2:2]
    slack = jnp.minimum(sizes[donor] - 1, most - sizes[sink]) // 2
    slack = jnp.where((donor == ranking[0]) | (sink == ranking[0]) | (sizes[sink] == 0), 0, jnp.maximum(slack, 0))
    passed = jax.random.randint(jax.random.fold_in(own, 4), (number_of // 2,), 0, 1 << 20) % (slack + 1)
    sizes = sizes.at[donor].add(-passed).at[sink].add(passed)
    members = jnp.searchsorted(jnp.cumsum(sizes), jnp.arange(rows * top), side="right").astype(jnp.int32)
    grid = members.reshape(top, rows).T
    grid = grid[jax.random.permutation(jax.random.fold_in(own, 1), rows)]
    offset_by = jax.random.randint(jax.random.fold_in(own, 2), (rows, 1), 0, top)
    return jnp.take_along_axis(grid, (jnp.arange(top)[None, :] + offset_by) % top, axis=1)


def load_shares(count, total, limit, slope, full):
    weights = [(1 << 20) // math.isqrt(standing ** slope) + 1 for standing in range(1, count + 1)]
    largest = limit if full else min(limit, max(-(-total // count), total * weights[0] // sum(weights)))
    least = 1 if total - largest >= count - 1 else 0
    holding, surplus = [largest] + [least] * (count - 1), total - largest - least * (count - 1)
    while surplus > 0:
        candidates = [i for i in range(1, count) if holding[i] < largest] or [i for i in range(1, count) if holding[i] < limit]
        pool, budget = sum([weights[i] for i in candidates]), surplus
        for i in candidates:
            more = min(limit - holding[i], max(1, budget * weights[i] // pool), surplus)
            holding[i] = holding[i] + more
            surplus = surplus - more
    return np.array(holding)


def noise(own_key, extent, scale, reach, pieces=(), dtype=jnp.bfloat16):
    entries = jax.random.normal(own_key, extent, jnp.float32) * scale
    if len(pieces) > 0:
        entries = shard_levels(own_key, extent, pieces, -0.22, 0.18) * entries
    return jnp.clip(entries, min=-reach, max=reach).astype(dtype)


def setup_inputs(seed: int = 0) -> dict:
    seeds = jax.random.split(jax.random.key(seed), 12)
    acts_fwd = noise(seeds[0], (SECTIONS, TOKENS, D), 1.0, 6.0, ((0, 8), (1, 128)))
    ids_fwd_keys = jax.random.split(jax.random.fold_in(seeds[1], 1), SECTIONS * TOKENS // TOK_DEV)
    ids_fwd_turns = jax.random.permutation(jax.random.fold_in(seeds[1], 3), SECTIONS * TOKENS // TOK_DEV)
    ids_fwd = jax.vmap(lambda own, number: routed_block(jax.random.fold_in(seeds[1], 2), own, number, TOK_DEV, EXPERTS, TOP, CAP, 2))(ids_fwd_keys, ids_fwd_turns).reshape((SECTIONS, TOKENS, TOP))
    scores_fwd = jnp.clip(jnp.exp(math.log(0.95) - 2.944439 * jax.random.uniform(seeds[2], (SECTIONS, TOKENS, TOP), jnp.float32) ** shard_levels(seeds[2], (SECTIONS, TOKENS, TOP), ((0, 8), (1, 128)), -0.2, 0.2)), 0.05, 0.95)
    cot_bwd = noise(seeds[3], (SECTIONS, TOKENS, D), 0.25, 1.5, ((0, 8), (1, 128)))
    ids_bwd_keys = jax.random.split(jax.random.fold_in(seeds[4], 1), SECTIONS * TOKENS // TOK_DEV)
    ids_bwd_turns = jax.random.permutation(jax.random.fold_in(seeds[4], 3), SECTIONS * TOKENS // TOK_DEV)
    ids_bwd = jax.vmap(lambda own, number: routed_block(jax.random.fold_in(seeds[4], 2), own, number, TOK_DEV, EXPERTS, TOP, CAP, 2))(ids_bwd_keys, ids_bwd_turns).reshape((SECTIONS, TOKENS, TOP))
    scores_bwd = jnp.clip(jnp.exp(math.log(0.95) - 2.944439 * jax.random.uniform(seeds[5], (SECTIONS, TOKENS, TOP), jnp.float32) ** shard_levels(seeds[5], (SECTIONS, TOKENS, TOP), ((0, 8), (1, 128)), -0.2, 0.2)), 0.05, 0.95)
    saved_out = noise(seeds[6], (SECTIONS, TOKENS, TOP, D), 0.25, 1.5, ((0, 8), (1, 128)))
    saved_pre = noise(seeds[7], (SECTIONS, ROWS, 2, EXPERTS * FE), 1.0, 6.0, ((0, 8), (1, 4), (3, 32)))
    w_gate = noise(seeds[8], (SECTIONS, D, EXPERTS * FE), D ** -0.5, 0.09375, ((0, 8), (2, 32)))
    w_up = noise(seeds[9], (SECTIONS, D, EXPERTS * FE), D ** -0.5, 0.09375, ((0, 8), (2, 32)))
    w_down = noise(seeds[10], (SECTIONS, EXPERTS * FE, D), FE ** -0.5, 0.125, ((0, 8), (1, 32)))
    return {"acts_fwd": acts_fwd, "ids_fwd": ids_fwd, "scores_fwd": scores_fwd, "cot_bwd": cot_bwd, "ids_bwd": ids_bwd, "scores_bwd": scores_bwd, "saved_out": saved_out, "saved_pre": saved_pre, "w_gate": w_gate, "w_up": w_up, "w_down": w_down}


def mix_weights(scores):
    return 2.5 * scores / jnp.sum(scores, axis=-1, keepdims=True)


def score_gradient(scores, dots):
    score_total = jnp.sum(scores, axis=-1, keepdims=True)
    return 2.5 / score_total * (dots - jnp.sum(dots * scores, axis=-1, keepdims=True) / score_total)


def slot_table(expert_ids):
    pair_count = TOK_DEV * TOP
    blocks = expert_ids.reshape(-1, pair_count)
    same_expert = blocks[:, :, None] == blocks[:, None, :]
    position = jnp.arange(pair_count).astype(jnp.int32)
    earlier = position[None, :] < position[:, None]
    slot_ids = jnp.sum(same_expert & earlier[None], axis=2).astype(jnp.int32)
    return slot_ids.reshape(expert_ids.shape)


def round_trip(values):
    return lax.optimization_barrier(values.astype(jnp.bfloat16)).astype(jnp.float32)


def expert_major(gate_w, up_w, down_w):
    width = gate_w.shape[0]
    gate_all = gate_w.reshape(width, EXPERTS, FE).transpose(1, 0, 2)
    up_all = up_w.reshape(width, EXPERTS, FE).transpose(1, 0, 2)
    down_all = down_w.reshape(EXPERTS, FE, width)
    return gate_all, up_all, down_all


def section_forward(packed):
    acts, expert_ids, scores, gate_w, up_w, down_w = packed
    weights = mix_weights(scores)
    group = N_EXPERT // EXPERTS
    units = FE // group
    width = acts.shape[1]
    gate_all, up_all, down_all = expert_major(gate_w, up_w, down_w)

    def one_expert(running, item):
        gate_slab, up_slab, down_slab, expert_index = item
        gate_pre = jnp.dot(acts, gate_slab, preferred_element_type=jnp.float32)
        up_pre = jnp.dot(acts, up_slab, preferred_element_type=jnp.float32)
        hidden = (gate_pre * jax.nn.sigmoid(gate_pre) * up_pre).astype(jnp.bfloat16)
        hidden32 = hidden.astype(jnp.float32).reshape(hidden.shape[0], group, units)
        down32 = down_slab.astype(jnp.float32).reshape(group, units, width)
        partial_value = jnp.einsum('tqf,qfd->tqd', hidden32, down32, precision=lax.Precision.HIGHEST)
        expert_out = jnp.sum(round_trip(partial_value), axis=1)
        coefficient = jnp.sum(jnp.where(expert_ids == expert_index, weights, 0.0), axis=-1)
        return running + coefficient[:, None] * expert_out, None

    experts = jnp.arange(EXPERTS).astype(jnp.int32)
    running, _ = lax.scan(one_expert, acts.astype(jnp.float32), (gate_all, up_all, down_all, experts))
    return running.astype(jnp.bfloat16)


def section_backward(packed):
    cot, expert_ids, scores, pre, gate_w, up_w, down_w = packed
    weights = mix_weights(scores)
    slot_ids = slot_table(expert_ids)
    group = N_EXPERT // EXPERTS
    units = FE // group
    width = cot.shape[1]
    token_count = cot.shape[0]
    token_index = jnp.arange(token_count).astype(jnp.int32)
    source = token_index // TOK_DEV
    row_base = ((source % N_DP) * N_EXPERT + source // N_DP) * CAP
    row_index = row_base[:, None] + slot_ids
    row_ids = jnp.arange(pre.shape[0]).astype(jnp.int32)
    cot32 = cot.astype(jnp.float32)
    gate_all, up_all, down_all = expert_major(gate_w, up_w, down_w)
    pre_all = pre.reshape(pre.shape[0], 2, EXPERTS, FE).transpose(2, 0, 1, 3)

    def one_expert(running, item):
        pre_expert, gate_slab, up_slab, down_slab, expert_index = item
        hit = expert_ids == expert_index
        coefficient = jnp.sum(jnp.where(hit, weights, 0.0), axis=-1)
        values = (coefficient[:, None] * cot32).astype(jnp.bfloat16)
        placer = jnp.sum(hit[None] & (row_index[None] == row_ids[:, None, None]), axis=-1).astype(jnp.float32)
        slot_rows = jnp.dot(placer, values.astype(jnp.float32), precision=lax.Precision.HIGHEST,
                            preferred_element_type=jnp.float32).astype(jnp.bfloat16)
        grad_hidden = lax.dot_general(slot_rows, down_slab, (((1,), (1,)), ((), ())),
                                      preferred_element_type=jnp.float32)
        gate_pre = pre_expert[:, 0].astype(jnp.float32)
        up_pre = pre_expert[:, 1].astype(jnp.float32)
        sigmoid_gate = jax.nn.sigmoid(gate_pre)
        grad_gate = (grad_hidden * up_pre * sigmoid_gate * (1.0 + gate_pre * (1.0 - sigmoid_gate))).astype(jnp.bfloat16)
        grad_up = (grad_hidden * gate_pre * sigmoid_gate).astype(jnp.bfloat16)
        hidden = (gate_pre * sigmoid_gate * up_pre).astype(jnp.bfloat16)
        row_total = grad_gate.shape[0]
        gate32 = gate_slab.astype(jnp.float32).reshape(width, group, units)
        up32 = up_slab.astype(jnp.float32).reshape(width, group, units)
        partial_value = jnp.einsum('rqf,dqf->rqd', grad_gate.astype(jnp.float32).reshape(row_total, group, units),
                             gate32, precision=lax.Precision.HIGHEST)
        partial_value = partial_value + jnp.einsum('rqf,dqf->rqd', grad_up.astype(jnp.float32).reshape(row_total, group, units),
                                       up32, precision=lax.Precision.HIGHEST)
        expert_rows = jnp.sum(round_trip(partial_value), axis=1)
        back = lax.dot_general(placer, expert_rows, (((0,), (0,)), ((), ())),
                               precision=lax.Precision.HIGHEST, preferred_element_type=jnp.float32)
        down_part = jnp.dot(slot_rows.T, hidden, preferred_element_type=jnp.float32)
        return running + back, down_part

    experts = jnp.arange(EXPERTS).astype(jnp.int32)
    running, down_parts = lax.scan(one_expert, cot32, (pre_all, gate_all, up_all, down_all, experts))
    down_grad = down_parts.transpose(1, 0, 2).reshape(width, EXPERTS * FE)
    return running.astype(jnp.bfloat16), down_grad


def reference(acts_fwd, ids_fwd, scores_fwd, cot_bwd, ids_bwd, scores_bwd, saved_out, saved_pre, w_gate, w_up, w_down):
    section_out = lax.map(section_forward, (acts_fwd, ids_fwd, scores_fwd, w_gate, w_up, w_down))
    section_grad, down_grad = lax.map(section_backward, (cot_bwd, ids_bwd, scores_bwd, saved_pre, w_gate, w_up, w_down))
    dots = jnp.einsum('stkd,std->stk', saved_out.astype(jnp.float32), cot_bwd.astype(jnp.float32),
                      precision=lax.Precision.HIGHEST)
    score_grads = score_gradient(scores_bwd, dots)
    zero_section = jnp.zeros_like(section_out[:1])
    acts_sent = jnp.concatenate([section_out[1:], zero_section], axis=0)
    grads_sent = jnp.concatenate([section_grad[1:], zero_section], axis=0)
    return acts_sent, grads_sent, score_grads, down_grad
```

```python
import functools

import jax
import jax.numpy as jnp
from jax import lax
from jax.experimental import pallas as pl
from jax.experimental.pallas import tpu as pltpu
from jax.sharding import PartitionSpec as P

FE = 2048
PIECES = 4
MESH = pl.DeviceIdType.MESH


def score_gradient(scores, dots):
    score_total = jnp.sum(scores, axis=-1, keepdims=True)
    return 2.5 / score_total * (dots - jnp.sum(dots * scores, axis=-1, keepdims=True) / score_total)


def column(row):
    n = row.shape[1]
    i = lax.broadcasted_iota(jnp.int32, (n, n), 0)
    j = lax.broadcasted_iota(jnp.int32, (n, n), 1)
    return jnp.sum(jnp.where(i == j, jnp.broadcast_to(row, (n, n)), 0.0), axis=1, keepdims=True)


def routing_rows(ids_t, scores_t, with_slots):
    ids = ids_t.astype(jnp.float32)
    weights = 2.5 * scores_t / jnp.sum(scores_t, axis=0, keepdims=True)
    tokens = ids.shape[1]
    lane = lax.broadcasted_iota(jnp.int32, (tokens, 128), 1).astype(jnp.float32)
    coefficient = jnp.zeros((tokens, 128), jnp.float32)
    hit = jnp.zeros((tokens, 128), jnp.float32)
    for k in range(2):
        expert = column(ids[k : k + 1])
        coefficient = coefficient + jnp.where(expert == lane, column(weights[k : k + 1]), 0.0)
        hit = hit + jnp.where(expert + 8.0 == lane, 1.0, 0.0)
    slots = jnp.full((tokens, 128), -1.0, jnp.float32)
    if with_slots:
        running = jnp.zeros((1, 128), jnp.float32)
        before = []
        for t in range(tokens):
            before.append(running)
            running = running + hit[t : t + 1]
        slots = jnp.where(hit > 0.0, jnp.concatenate(before, axis=0), -1.0)
    return jnp.where(lane < 8.0, coefficient, slots)


def dot(a, b):
    return jnp.dot(a, b, preferred_element_type=jnp.float32)


def dot_nt(a, b):
    return lax.dot_general(a, b, (((1,), (1,)), ((), ())), preferred_element_type=jnp.float32)


def dot_tn(a, b):
    return lax.dot_general(a, b, (((0,), (0,)), ((), ())), preferred_element_type=jnp.float32)


def kernel(
    n_pipe, n_dev, n_dp, group,
    acts_ref, cot_ref, ids_fwd_ref, scores_fwd_ref, ids_bwd_ref, scores_bwd_ref, pre_ref,
    wg_hbm, wu_hbm, wd_hbm,
    acts_out, grads_out, down_out,
    x, meta, wg, wu, wd, gate_acc, up_acc, gh_acc, placer, hid, sc, sc_send,
    sib_send, sib_recv, own, rs_send, rs_recv, fin_send, fin_recv,
    w_sem, ag_recv, ag_ring, ag_sib, hid_s, hid_r, sc_s, sc_r,
    sib_s, sib_r, rs_s, rs_r, fin_s, fin_r,
):
    n_chip = n_dev // 2
    half = n_chip // 2
    pipe = lax.axis_index("pipe")
    me = lax.axis_index("expert")
    mine_dp = lax.axis_index("dp")
    z, core = lax.div(me, 2), lax.rem(me, 2)
    sib = z * 2 + 1 - core
    right = lax.rem(z + 1, n_chip) * 2 + core
    left = lax.rem(z + n_chip - 1, n_chip) * 2 + core
    before, after = lax.rem(pipe + n_pipe - 1, n_pipe), lax.rem(pipe + 1, n_pipe)
    expert = lax.div(me, group)
    rows = n_dev * 8
    width = x.shape[3]
    slots = pre_ref.shape[1]
    cap = slots // n_dev

    def remote(src, dst, send_sem, recv_sem, **where):
        return pltpu.make_async_remote_copy(
            src_ref=src, dst_ref=dst, send_sem=send_sem, recv_sem=recv_sem,
            device_id=where, device_id_type=MESH,
        )

    barrier = pltpu.get_barrier_semaphore()
    peers = [dict(expert=right), dict(expert=left), dict(expert=sib)]
    peers += [dict(dp=lax.rem(mine_dp + r, n_dp)) for r in range(1, n_dp)]
    peers += [dict(pipe=p, expert=d) for p in (before, after) for d in (me, sib)]
    for peer in peers:
        pl.semaphore_signal(barrier, inc=1, device_id=peer, device_id_type=MESH)

    loads = []
    for q in range(PIECES):
        loads.append((
            pltpu.make_async_copy(wg_hbm.at[q], wg.at[q], w_sem.at[0, q]),
            pltpu.make_async_copy(wu_hbm.at[q], wu.at[q], w_sem.at[1, q]),
            pltpu.make_async_copy(wd_hbm.at[:, pl.ds(q * width, width)], wd.at[q], w_sem.at[2, q]),
        ))
        for load in loads[-1]:
            load.start()

    for q in range(PIECES):
        part = pl.ds(q * width, width)
        x[q, me] = jnp.concatenate(
            [acts_ref[:, part].astype(jnp.float32), cot_ref[:, part].astype(jnp.float32)], axis=0
        ).astype(jnp.bfloat16)
    meta[me] = jnp.concatenate(
        [
            routing_rows(ids_fwd_ref[...], scores_fwd_ref[...], False),
            routing_rows(ids_bwd_ref[...], scores_bwd_ref[...], True),
        ],
        axis=0,
    )
    gate_pre = pre_ref[0].astype(jnp.float32)
    up_pre = pre_ref[1].astype(jnp.float32)
    hid[n_dp - 1] = (gate_pre * jax.nn.sigmoid(gate_pre) * up_pre).astype(jnp.bfloat16)

    pl.semaphore_wait(barrier, len(peers))

    def block(q, d):
        return meta.at[d] if q == PIECES else x.at[q, d]

    order = (PIECES,) + tuple(range(PIECES))

    def hop(q, d, to, sem):
        return remote(block(q, d), block(q, d), sem, ag_recv.at[q, d], expert=to)

    def gather_wait(q, d):
        hop(q, d, sib, ag_sib.at[q, 0]).wait_recv()

    def gather_step(s, forward_plus, forward_minus, minus):
        plus_d = lax.rem(z + n_chip - s, n_chip) * 2 + core
        minus_d = lax.rem(z + s, n_chip) * 2 + core
        for q in order:
            gather_wait(q, plus_d)
            if forward_plus:
                hop(q, plus_d, right, ag_ring.at[q, 0, s]).start()
            hop(q, plus_d, sib, ag_sib.at[q, s]).start()
            if minus:
                gather_wait(q, minus_d)
                if forward_minus:
                    hop(q, minus_d, left, ag_ring.at[q, 1, s]).start()
                hop(q, minus_d, sib, ag_sib.at[q, n_chip - s]).start()

    for q in order:
        hop(q, me, right, ag_ring.at[q, 0, 0]).start()
        hop(q, me, left, ag_ring.at[q, 1, 0]).start()
        hop(q, me, sib, ag_sib.at[q, 0]).start()
    hid_copies = []
    for r in range(1, n_dp):
        hid_copies.append(remote(
            hid.at[n_dp - 1], hid.at[r - 1], hid_s.at[r - 1], hid_r.at[r - 1],
            dp=lax.rem(mine_dp + r, n_dp),
        ))
        hid_copies[-1].start()

    def gather_body(s, carry):
        gather_step(s, True, True, True)
        return carry

    lax.fori_loop(1, half - 1, gather_body, 0)
    gather_step(half - 1, True, False, True)
    gather_step(half, False, False, False)

    def sibling_wait(q):
        def body(i, carry):
            gather_wait(q, i * 2 + 1 - core)
            return carry

        lax.fori_loop(0, n_chip, body, 0)

    sibling_wait(PIECES)
    table = meta[...].reshape(rows, 128)
    lane = lax.broadcasted_iota(jnp.int32, (rows, 128), 1)
    coefficient = jnp.sum(jnp.where(lane == expert, table, 0.0), axis=1, keepdims=True)
    slot = jnp.sum(jnp.where(lane == expert + 8, table, 0.0), axis=1, keepdims=True)
    row = lax.broadcasted_iota(jnp.int32, (rows, 1), 0)
    forward_row = (row & 7) < 4
    target = jnp.where(slot < 0.0, -1.0, slot + (cap * (row >> 3)).astype(jnp.float32))
    column_ids = lax.broadcasted_iota(jnp.int32, (rows, slots), 1).astype(jnp.float32)
    placer[...] = jnp.where(column_ids == target, 1.0, 0.0).astype(jnp.bfloat16)

    for q in range(PIECES):
        sibling_wait(q)
        for load in loads[q]:
            load.wait()
        xq = x[q].reshape(rows, width)
        scaled = (coefficient * xq.astype(jnp.float32)).astype(jnp.bfloat16)
        g, u, h = dot(xq, wg[q]), dot(xq, wu[q]), dot_nt(scaled, wd[q])
        if q == 0:
            gate_acc[...], up_acc[...], gh_acc[...] = g, u, h
        else:
            gate_acc[...] += g
            up_acc[...] += u
            gh_acc[...] += h
        sc_send[q] = dot_tn(placer[...], scaled).astype(jnp.bfloat16)

    sc_copies = []
    for r in range(1, n_dp):
        peer = lax.rem(mine_dp + r, n_dp)
        sc_copies.append(remote(sc_send.at[peer], sc.at[r - 1], sc_s.at[r - 1], sc_r.at[r - 1], dp=peer))
        sc_copies[-1].start()

    gate = gate_acc[...]
    hidden = jnp.where(forward_row, gate * jax.nn.sigmoid(gate) * up_acc[...], 0.0).astype(jnp.bfloat16)
    gate_b = dot(placer[...], pre_ref[0])
    up_b = dot(placer[...], pre_ref[1])
    sg = jax.nn.sigmoid(gate_b)
    grad_hidden = jnp.where(forward_row, 0.0, gh_acc[...])
    grad_gate = (grad_hidden * up_b * sg * (1.0 + gate_b * (1.0 - sg))).astype(jnp.bfloat16)
    grad_up = (grad_hidden * gate_b * sg).astype(jnp.bfloat16)
    scale = jnp.where(forward_row, coefficient, 1.0)

    def output_piece(q):
        value = dot(hidden, wd[q]) + dot_nt(grad_gate, wg[q]) + dot_nt(grad_up, wu[q])
        return (scale * value).reshape(n_chip, 16, width)

    sib_copies = []
    for k in range(2):
        sib_send[k] = output_piece((1 - core) * 2 + k).astype(jnp.bfloat16)
        sib_copies.append(remote(sib_send.at[k], sib_recv.at[k], sib_s.at[k], sib_r.at[k], expert=sib))
        sib_copies[-1].start()
        own[k] = output_piece(core * 2 + k)

    def local(k, d):
        return own[k, d] + sib_recv[k, d].astype(jnp.float32)

    def ring_copy(k, way, s):
        return remote(
            rs_send.at[k, way, s], rs_recv.at[k, way, s], rs_s.at[k, way, s], rs_r.at[k, way, s],
            expert=right if way == 0 else left,
        )

    def send_sum(k, way, s, value):
        rs_send[k, way, s] = value.astype(jnp.bfloat16)
        ring_copy(k, way, s).start()

    for k in range(2):
        sib_copies[k].wait_recv()
        send_sum(k, 0, 0, local(k, lax.rem(z + half, n_chip)))
        send_sum(k, 1, 0, local(k, lax.rem(z + half + 1, n_chip)))

    def pass_on(k, way, s):
        ring_copy(k, way, s).wait_recv()
        d = z + half - 1 - s if way == 0 else z + half + 2 + s
        value = rs_recv[k, way, s].astype(jnp.float32) + local(k, lax.rem(d, n_chip))
        send_sum(k, way, s + 1, value)

    def ring_body(s, carry):
        for k in range(2):
            for way in range(2):
                pass_on(k, way, s)
        return carry

    lax.fori_loop(0, half - 2, ring_body, 0)
    fin_copies = []
    for k in range(2):
        pass_on(k, 0, half - 2)
    for k in range(2):
        ring_copy(k, 1, half - 2).wait_recv()
        ring_copy(k, 0, half - 1).wait_recv()
        value = local(k, z) + rs_recv[k, 1, half - 2].astype(jnp.float32)
        value = value + rs_recv[k, 0, half - 1].astype(jnp.float32)
        start = x[core * 2 + k, pl.ds(z * 2, 2)].reshape(16, width)
        fin_send[k] = (start.astype(jnp.float32) + value).astype(jnp.bfloat16).reshape(2, 8, width)
        for i in range(2):
            q = core * 2 + k
            fin_copies.append(remote(
                fin_send.at[k, i], fin_recv.at[q], fin_s.at[k, i], fin_r.at[q],
                pipe=before, expert=z * 2 + i,
            ))
            fin_copies[-1].start()

    sc[n_dp - 1] = sc_send[mine_dp]
    for copy in hid_copies + sc_copies:
        copy.wait_recv()
    down_out[...] = dot_tn(sc[...].reshape(n_dp * slots, width), hid[...].reshape(n_dp * slots, hid.shape[2]))

    last = pipe == n_pipe - 1
    for q in range(PIECES):
        remote(fin_send.at[0, 0], fin_recv.at[q], fin_s.at[0, 0], fin_r.at[q], expert=sib).wait_recv()
        value = jnp.where(last, 0.0, fin_recv[q].astype(jnp.float32)).astype(jnp.bfloat16)
        acts_out[:, pl.ds(q * width, width)] = value[0:4]
        grads_out[:, pl.ds(q * width, width)] = value[4:8]

    for copy in hid_copies + sc_copies + sib_copies + fin_copies:
        copy.wait_send()
    for k in range(2):
        for way in range(2):
            for s in range(half - way):
                ring_copy(k, way, s).wait_send()
    for q in order:
        for way in range(2):
            for s in range(half - way):
                hop(q, me, right, ag_ring.at[q, way, s]).wait_send()
        for s in range(n_chip):
            hop(q, me, sib, ag_sib.at[q, s]).wait_send()


def shards(
    acts_fwd, ids_fwd, scores_fwd, cot_bwd, ids_bwd, scores_bwd, saved_out, saved_pre, w_gate, w_up, w_down,
):
    n_pipe, n_dev, n_dp = lax.axis_size("pipe"), lax.axis_size("expert"), lax.axis_size("dp")
    model, units = w_gate.shape[1:]
    slots = saved_pre.shape[1]
    width = model // PIECES
    n_chip = n_dev // 2
    half = n_chip // 2
    rows = n_dev * 8
    bf16, f32 = jnp.bfloat16, jnp.float32
    vmem = pl.BlockSpec(memory_space=pltpu.VMEM)
    hbm = pl.BlockSpec(memory_space=pl.ANY)
    dma = pltpu.SemaphoreType.DMA
    scratch = [
        pltpu.VMEM((PIECES, n_dev, 8, width), bf16),
        pltpu.VMEM((n_dev, 8, 128), f32),
        pltpu.VMEM((PIECES, width, units), bf16),
        pltpu.VMEM((PIECES, width, units), bf16),
        pltpu.VMEM((PIECES, units, width), bf16),
        pltpu.VMEM((rows, units), f32),
        pltpu.VMEM((rows, units), f32),
        pltpu.VMEM((rows, units), f32),
        pltpu.VMEM((rows, slots), bf16),
        pltpu.VMEM((n_dp, slots, units), bf16),
        pltpu.VMEM((n_dp, slots, width), bf16),
        pltpu.VMEM((n_dp, slots, width), bf16),
        pltpu.VMEM((2, n_chip, 16, width), bf16),
        pltpu.VMEM((2, n_chip, 16, width), bf16),
        pltpu.VMEM((2, n_chip, 16, width), f32),
        pltpu.VMEM((2, 2, half, 16, width), bf16),
        pltpu.VMEM((2, 2, half, 16, width), bf16),
        pltpu.VMEM((2, 2, 8, width), bf16),
        pltpu.VMEM((PIECES, 8, width), bf16),
        dma((3, PIECES)),
        dma((PIECES + 1, n_dev)),
        dma((PIECES + 1, 2, half)),
        dma((PIECES + 1, n_chip)),
        dma((n_dp - 1,)), dma((n_dp - 1,)), dma((n_dp - 1,)), dma((n_dp - 1,)),
        dma((2,)), dma((2,)),
        dma((2, 2, half)), dma((2, 2, half)),
        dma((2, 2)), dma((PIECES,)),
    ]
    acts_sent, grads_sent, down_grad = pl.pallas_call(
        functools.partial(kernel, n_pipe, n_dev, n_dp, FE // units),
        out_shape=(
            jax.ShapeDtypeStruct(acts_fwd.shape[1:], bf16),
            jax.ShapeDtypeStruct(acts_fwd.shape[1:], bf16),
            jax.ShapeDtypeStruct((width, units), f32),
        ),
        in_specs=[vmem] * 7 + [hbm] * 3,
        out_specs=(vmem, vmem, vmem),
        scratch_shapes=scratch,
        compiler_params=pltpu.CompilerParams(
            collective_id=0, has_side_effects=True, vmem_limit_bytes=56 * 1024 * 1024
        ),
        name="relay_layer",
    )(
        acts_fwd[0], cot_bwd[0], ids_fwd[0].T, scores_fwd[0].T, ids_bwd[0].T, scores_bwd[0].T,
        saved_pre[0].transpose(1, 0, 2),
        w_gate[0].reshape(PIECES, width, units), w_up[0].reshape(PIECES, width, units), w_down[0],
    )
    dots = jnp.einsum("tkd,td->tk", saved_out[0], cot_bwd[0], preferred_element_type=jnp.float32)
    score_grads = score_gradient(scores_bwd[0], dots)
    return (acts_sent[None], grads_sent[None], score_grads[None], down_grad[None])


def solution(mesh):
    token_spec = P("pipe", ("expert", "dp"), None)
    in_specs = (
        token_spec, token_spec, token_spec, token_spec, token_spec, token_spec,
        P("pipe", ("expert", "dp"), None, None),
        P("pipe", "dp", None, "expert"),
        P("pipe", None, "expert"),
        P("pipe", None, "expert"),
        P("pipe", "expert", None),
    )
    out_specs = (token_spec, token_spec, token_spec, P("pipe", "dp", "expert"))
    return jax.shard_map(shards, mesh=mesh, in_specs=in_specs, out_specs=out_specs, check_vma=False)
```

```python
import functools

import jax
import jax.numpy as jnp
from jax import lax
from jax.experimental import pallas as pl
from jax.experimental.pallas import tpu as pltpu
from jax.sharding import PartitionSpec as P

FE = 2048
ROUTE = (
    (0, None), (1, 0), (-1, 0), (3, 0), (-3, 0), (2, 3), (-2, 4), (4, 3), (-4, 4), (6, 3), (-6, 4),
    (5, 9), (-5, 10), (7, 9), (-7, 10), (8, 9),
)
LANES = 128
MESH = pl.DeviceIdType.MESH
BF16, F32 = jnp.bfloat16, jnp.float32


def column(row):
    n = row.shape[1]
    i = lax.broadcasted_iota(jnp.int32, (n, n), 0)
    j = lax.broadcasted_iota(jnp.int32, (n, n), 1)
    return jnp.sum(jnp.where(i == j, jnp.broadcast_to(row, (n, n)), 0.0), axis=1, keepdims=True)


def routing_rows(ids_t, scores_t, with_slots):
    ids = ids_t.astype(F32)
    weights = 2.5 * scores_t / jnp.sum(scores_t, axis=0, keepdims=True)
    tokens = ids.shape[1]
    lane = lax.broadcasted_iota(jnp.int32, (tokens, LANES), 1)
    lane_expert = (lane & 3).astype(F32)
    weight = jnp.zeros((tokens, LANES), F32)
    hit = jnp.zeros((tokens, LANES), F32)
    for k in range(2):
        match = column(ids[k : k + 1]) == lane_expert
        weight = weight + jnp.where(match, column(weights[k : k + 1]), 0.0)
        hit = hit + jnp.where(match, 1.0, 0.0)
    slots = jnp.full((tokens, LANES), -1.0, F32)
    if with_slots:
        running = jnp.zeros((1, LANES), F32)
        before = []
        for t in range(tokens):
            before.append(running)
            running = running + hit[t : t + 1]
        slots = jnp.where(hit > 0.0, jnp.concatenate(before, axis=0), -1.0)
    high = weight.astype(BF16).astype(F32)
    middle = (weight - high).astype(BF16).astype(F32)
    low = weight - high - middle
    return jnp.where(lane < 4, high, jnp.where(lane < 8, middle, jnp.where(lane < 12, low, slots)))


def dot(a, b):
    return jnp.dot(a, b, preferred_element_type=F32)


def dot_nt(a, b):
    return lax.dot_general(a, b, (((1,), (1,)), ((), ())), preferred_element_type=F32)


def dot_tn(a, b):
    return lax.dot_general(a, b, (((0,), (0,)), ((), ())), preferred_element_type=F32)


def kernel(
    n_pipe, n_dev, n_dp, group,
    acts_hbm, cot_hbm, ids_fwd_hbm, scores_fwd_hbm, ids_bwd_hbm, scores_bwd_hbm,
    pre_hbm, saved_hbm, wg_hbm, wu_hbm, wd_hbm,
    fin_recv, sc, hid, sg_out,
    acts_ref, cot_ref, ids_fwd_ref, scores_fwd_ref, ids_bwd_ref, scores_bwd_ref,
    x, wg, wu, wd, pre_in, saved, pre, coef, scale, placer, scaled, gate_acc, up_acc, gh_acc,
    hid_b, gg_b, gu_b, sc_send, sib_send, sib_recv, own, rs_send, rs_recv, fin_send,
    small_sem, w_sem, in_sem, ag_recv, ag_send, ag_sib, hid_s, hid_r, sc_s, sc_r,
    sib_s, sib_r, rs_s, rs_r, fin_s, fin_r,
):
    n_chip = n_dev // 2
    half = n_chip // 2
    pipe = lax.axis_index("pipe")
    me = lax.axis_index("expert")
    mine_dp = lax.axis_index("dp")
    z, core = lax.div(me, 2), lax.rem(me, 2)
    sib = z * 2 + 1 - core
    before, after = lax.rem(pipe + n_pipe - 1, n_pipe), lax.rem(pipe + 1, n_pipe)
    expert = lax.div(me, group)
    tiles = x.shape[2]
    piece = rs_send.shape[3]
    per_piece = piece // LANES
    per_half = 2 * per_piece
    model = 4 * piece
    slots = pre_in.shape[0]
    cap = slots // n_dev
    batch = half * 16
    bslots = half * 2 * cap

    edges = [(c, ROUTE[c][1]) for c in range(1, n_chip)]

    def chip_at(step):
        return lax.rem(z + step + n_chip, n_chip) * 2 + core

    def remote(src, dst, send_sem, recv_sem, **where):
        return pltpu.make_async_remote_copy(
            src_ref=src, dst_ref=dst, send_sem=send_sem, recv_sem=recv_sem,
            device_id=where, device_id_type=MESH,
        )

    small = [
        pltpu.make_async_copy(source, target, small_sem.at[i])
        for i, (source, target) in enumerate((
            (acts_hbm, acts_ref), (cot_hbm, cot_ref), (ids_fwd_hbm, ids_fwd_ref),
            (scores_fwd_hbm, scores_fwd_ref), (ids_bwd_hbm, ids_bwd_ref), (scores_bwd_hbm, scores_bwd_ref),
        ))
    ]
    for copy in small:
        copy.start()
    barrier = pltpu.get_barrier_semaphore()
    peers = [dict(expert=chip_at(step)) for step in sorted(set(ROUTE[c][0] - ROUTE[p][0] for c, p in edges)
             | set(ROUTE[p][0] - ROUTE[c][0] for c, p in edges))]
    peers += [dict(expert=sib)]
    peers += [dict(dp=lax.rem(mine_dp + r, n_dp)) for r in range(1, n_dp)]
    peers += [dict(pipe=p, expert=d) for p in (before, after) for d in (me, sib)]
    for peer in peers:
        pl.semaphore_signal(barrier, inc=1, device_id=peer, device_id_type=MESH)

    side = [pltpu.make_async_copy(pre_hbm, pre_in, in_sem.at[0]), pltpu.make_async_copy(saved_hbm, saved, in_sem.at[1])]
    loads = []
    for q in range(2):
        cols = pl.ds(q * 2 * piece, 2 * piece)
        loads += [
            pltpu.make_async_copy(wg_hbm.at[q], wg.at[q], w_sem.at[0, q]),
            pltpu.make_async_copy(wu_hbm.at[q], wu.at[q], w_sem.at[1, q]),
            pltpu.make_async_copy(wd_hbm.at[:, cols], wd.at[q], w_sem.at[2, q]),
        ]
    for load in side + loads:
        load.start()

    for copy in small:
        copy.wait()
    x[0, 0, 0] = jnp.concatenate(
        [
            routing_rows(ids_fwd_ref[...], scores_fwd_ref[...], False),
            routing_rows(ids_bwd_ref[...], scores_bwd_ref[...], True),
        ],
        axis=0,
    ).astype(BF16)
    for t in range(tiles - 1):
        part = pl.ds(t * LANES, LANES)
        x[0, 0, 1 + t] = jnp.concatenate([acts_ref[:, part].astype(F32), cot_ref[:, part].astype(F32)], axis=0).astype(BF16)

    pl.semaphore_wait(barrier, len(peers))

    def pass_rows(c):
        p = ROUTE[c][1]
        return remote(
            x.at[p, 0], x.at[c, 0], ag_send.at[c], ag_recv.at[c, 0], expert=chip_at(ROUTE[c][0] - ROUTE[p][0])
        )

    def pass_children(p):
        for c, parent in edges:
            if parent == p:
                pass_rows(c).start()

    def sib_rows(p):
        return remote(x.at[p, 0], x.at[p, 1], ag_sib.at[p], ag_recv.at[p, 1], expert=sib)

    for c in (3, 4, 1, 2):
        pass_rows(c).start()
    sib_rows(0).start()

    def take_rows(*places):
        for p in places:
            pass_rows(p).wait_recv()
            pass_children(p)
            sib_rows(p).start()

    def local_inputs():
        for copy in side:
            copy.wait()
        both = pre_in[...].astype(F32)
        gate_pre, up_pre = both[:, 0, :], both[:, 1, :]
        pre[0], pre[1] = gate_pre.astype(BF16), up_pre.astype(BF16)
        rows = (gate_pre * jax.nn.sigmoid(gate_pre) * up_pre).astype(BF16)
        i = lax.broadcasted_iota(jnp.int32, (slots, slots), 0)
        j = lax.broadcasted_iota(jnp.int32, (slots, slots), 1)
        chip, other, slot = lax.div(i, 2 * cap), lax.rem(lax.div(i, cap), 2), lax.rem(i, cap)
        wanted = origin(chip, other) * cap + slot
        swap = jnp.where(j == wanted, 1.0, 0.0).astype(BF16)
        hid[n_dp - 1] = dot(swap, rows).astype(BF16)

    def origin(p, other):
        step = jnp.zeros_like(p)
        for i in range(n_chip):
            step = jnp.where(p == i, ROUTE[i][0], step)
        chip = lax.rem(z - step + n_chip, n_chip)
        return chip * 2 + jnp.where(other == 0, core, 1 - core)

    def hid_copy(r):
        return remote(
            hid.at[n_dp - 1], hid.at[r - 1], hid_s.at[r - 1], hid_r.at[r - 1], dp=lax.rem(mine_dp + r, n_dp)
        )

    def score_gradients():
        scores = scores_bwd_ref[...]
        token = lax.broadcasted_iota(jnp.int32, scores.shape, 1)
        dots = jnp.zeros(scores.shape, F32)
        for t in range(scores.shape[1]):
            product = saved[t].astype(F32) * cot_ref[t : t + 1, :].astype(F32)
            dots = dots + jnp.where(token == t, jnp.sum(product, axis=1, keepdims=True), 0.0)
        total = jnp.sum(scores, axis=0, keepdims=True)
        sg_out[...] = 2.5 / total * (dots - jnp.sum(dots * scores, axis=0, keepdims=True) / total)

    def tile_rows(b, t):
        return x[b * half : (b + 1) * half, :, t].reshape(batch, LANES)

    def half_rows(b, q):
        return jnp.concatenate([tile_rows(b, 1 + q * per_half + t) for t in range(per_half)], axis=1)

    def is_forward(shape):
        return (lax.broadcasted_iota(jnp.int32, shape, 0) & 7) < 4

    def route(b):
        for p in range(b * half, (b + 1) * half):
            sib_rows(p).wait_recv()
        table = tile_rows(b, 0).astype(F32)
        lane = lax.broadcasted_iota(jnp.int32, (batch, LANES), 1)
        mine = (lane < 12) & ((lane & 3) == expert)
        weight = jnp.sum(jnp.where(mine, table, 0.0), axis=1, keepdims=True)
        slot = jnp.sum(jnp.where(lane == expert + 12, table, 0.0), axis=1, keepdims=True)
        coef[b] = jnp.broadcast_to(weight, (batch, LANES))
        scale[b] = jnp.where(is_forward((batch, LANES)), coef[b], 1.0)
        row = lax.broadcasted_iota(jnp.int32, (batch, 1), 0)
        device = origin(b * half + (row >> 4), (row >> 3) & 1)
        target = jnp.where(slot < 0.0, -1.0, slot + (cap * device).astype(F32))
        ids = lax.broadcasted_iota(jnp.int32, (batch, slots), 1).astype(F32)
        placer[b] = jnp.where(ids == target, 1.0, 0.0).astype(BF16)
        weights = coef[b]
        for t in range(tiles - 1):
            scaled[b, :, t * LANES : (t + 1) * LANES] = (weights * tile_rows(b, 1 + t).astype(F32)).astype(BF16)
        near = jnp.where(slot < 0.0, -1.0, slot + (cap * (row >> 3)).astype(F32))
        near_ids = lax.broadcasted_iota(jnp.int32, (batch, bslots), 1).astype(F32)
        near_placer = jnp.where(near_ids == near, 1.0, 0.0).astype(BF16)
        for q in range(4):
            part = scaled[b, :, q * piece : (q + 1) * piece]
            sc_send[q, b] = dot_tn(near_placer, part).astype(BF16)
        for r in range(1, n_dp):
            sc_copy(r, b).start()

    def sc_copy(r, b):
        peer = lax.rem(mine_dp + r, n_dp)
        return remote(sc_send.at[peer, b], sc.at[r - 1, b], sc_s.at[r - 1, b], sc_r.at[r - 1, b], dp=peer)

    def gate_up(b, q):
        rows = half_rows(b, q)
        g, u = dot(rows, wg[q]), dot(rows, wu[q])
        if q == 0:
            gate_acc[b], up_acc[b] = g, u
        else:
            gate_acc[b] += g
            up_acc[b] += u

    def grad_in(b):
        value = None
        for q in range(2):
            term = dot_nt(scaled[b, :, q * 2 * piece : (q + 1) * 2 * piece], wd[q])
            value = term if value is None else value + term
        gh_acc[b] = value

    def activate(b):
        forward = is_forward((batch, 1))
        gate = gate_acc[b]
        hid_b[b] = jnp.where(forward, gate * jax.nn.sigmoid(gate) * up_acc[b], 0.0).astype(BF16)
        gate_pre = dot(placer[b], pre[0])
        up_pre = dot(placer[b], pre[1])
        sg = jax.nn.sigmoid(gate_pre)
        grad_hidden = jnp.where(forward, 0.0, gh_acc[b])
        gg_b[b] = (grad_hidden * up_pre * sg * (1.0 + gate_pre * (1.0 - sg))).astype(BF16)
        gu_b[b] = (grad_hidden * gate_pre * sg).astype(BF16)

    def output(b, q, k):
        part = slice(k * piece, (k + 1) * piece)
        value = dot(hid_b[b], wd[q, :, part]) + dot_nt(gg_b[b], wg[q, part, :]) + dot_nt(gu_b[b], wu[q, part, :])
        return scale[b][:, 0:1] * value

    def sib_copy(k, b):
        span = pl.ds(b * half, half)
        return remote(sib_send.at[k, span], sib_recv.at[k, span], sib_s.at[k, b], sib_r.at[k, b], expert=sib)

    def output_sib(b, k):
        value = output(b, 1 - core, k).reshape(half, 2, 8, piece).astype(BF16)
        sib_send[k, b * half : (b + 1) * half, 0] = value[:, 1]
        sib_send[k, b * half : (b + 1) * half, 1] = value[:, 0]
        sib_copy(k, b).start()

    def output_own(b, k):
        own[k, b * half : (b + 1) * half] = output(b, core, k).reshape(half, 16, piece)

    def sib_wait(b):
        for k in range(2):
            sib_copy(k, b).wait_recv()

    def pass_sum(c):
        p = ROUTE[c][1]
        return remote(
            rs_send.at[c], rs_recv.at[c], rs_s.at[c], rs_r.at[c], expert=chip_at(ROUTE[p][0] - ROUTE[c][0])
        )

    def total(p, k):
        value = own[k, p] + sib_recv[k, p].astype(F32).reshape(16, piece)
        for c, parent in edges:
            if parent == p:
                value = value + rs_recv[c, k].astype(F32)
        return value

    def give_sums(*places):
        for p in places:
            for c, parent in edges:
                if parent == p:
                    pass_sum(c).wait_recv()
            for k in range(2):
                rs_send[p, k] = total(p, k).astype(BF16)
            pass_sum(p).start()

    local_inputs()
    for r in range(1, n_dp):
        hid_copy(r).start()
    take_rows(1, 2, 3, 4)
    score_gradients()
    take_rows(5, 6, 7, 8, 9, 10)
    route(0)
    take_rows(11, 12, 13, 14, 15)
    for load in loads:
        load.wait()
    gate_up(0, 0)
    gate_up(0, 1)
    route(1)
    gate_up(1, 0)
    gate_up(1, 1)
    grad_in(1)
    activate(1)
    output_sib(1, 0)
    output_sib(1, 1)
    output_own(1, 0)
    output_own(1, 1)
    sib_wait(1)
    give_sums(11, 12, 13, 14, 15)
    grad_in(0)
    activate(0)
    output_sib(0, 0)
    output_sib(0, 1)
    give_sums(9, 10)
    output_own(0, 0)
    output_own(0, 1)
    sib_wait(0)
    give_sums(5, 6, 7, 8, 1, 2)
    give_sums(3, 4)
    for c, parent in edges:
        if parent == 0:
            pass_sum(c).wait_recv()
    fin_copies = []
    for k in range(2):
        first = 1 + core * per_half + k * per_piece
        start = jnp.concatenate([x[0, :, first + t].reshape(16, LANES) for t in range(per_piece)], axis=1)
        fin_send[k] = (start.astype(F32) + total(0, k)).astype(BF16).reshape(2, 8, piece)
        for i in range(2):
            q = core * 2 + k
            fin_copies.append(remote(
                fin_send.at[k, i], fin_recv.at[q], fin_s.at[k, i], fin_r.at[q],
                pipe=before, expert=me if i == 0 else sib,
            ))
            fin_copies[-1].start()

    for b in range(2):
        sc[n_dp - 1, b] = sc_send[mine_dp, b]
    for r in range(1, n_dp):
        hid_copy(r).wait()
        for b in range(2):
            sc_copy(r, b).wait()
    for k in range(2):
        for b in range(2):
            sib_copy(k, b).wait_send()
    for c in range(1, n_chip):
        pass_rows(c).wait_send()
        pass_sum(c).wait_send()
    for p in range(n_chip):
        sib_rows(p).wait_send()
    for copy in fin_copies:
        copy.wait_send()
    for q in range(4):
        remote(fin_send.at[0, 0], fin_recv.at[q], fin_s.at[0, 0], fin_r.at[q], expert=sib).wait_recv()


def finish(n_pipe, fin, sc, hid, sg, acts_out, grads_out, sg_out, down_out):
    last = lax.axis_index("pipe") == n_pipe - 1
    pieces, _, piece = fin.shape
    for q in range(pieces):
        value = jnp.where(last, 0.0, fin[q].astype(F32)).astype(BF16)
        acts_out[:, q * piece : (q + 1) * piece] = value[0:4]
        grads_out[:, q * piece : (q + 1) * piece] = value[4:8]
    sg_out[...] = sg[...]
    rows = hid.shape[0] * hid.shape[1]
    down_out[...] = dot_tn(sc[...].reshape(rows, piece), hid[...].reshape(rows, hid.shape[2]))


def shards(
    acts_fwd, ids_fwd, scores_fwd, cot_bwd, ids_bwd, scores_bwd, saved_out, saved_pre, w_gate, w_up, w_down,
):
    n_pipe, n_dev, n_dp = lax.axis_size("pipe"), lax.axis_size("expert"), lax.axis_size("dp")
    model, units = w_gate.shape[1:]
    slots = saved_pre.shape[1]
    piece = model // 4
    n_chip = n_dev // 2
    half = n_chip // 2
    batch = half * 16
    bslots = slots // 2
    tiles = model // LANES + 1
    vmem = pl.BlockSpec(memory_space=pltpu.VMEM)
    hbm = pl.BlockSpec(memory_space=pltpu.HBM)
    dma = pltpu.SemaphoreType.DMA
    shape = jax.ShapeDtypeStruct
    scratch = [
        pltpu.VMEM(acts_fwd.shape[1:], BF16),
        pltpu.VMEM(acts_fwd.shape[1:], BF16),
        pltpu.VMEM((2, acts_fwd.shape[1]), jnp.int32),
        pltpu.VMEM((2, acts_fwd.shape[1]), F32),
        pltpu.VMEM((2, acts_fwd.shape[1]), jnp.int32),
        pltpu.VMEM((2, acts_fwd.shape[1]), F32),
        pltpu.VMEM((n_chip, 2, tiles, 8, LANES), BF16),
        pltpu.VMEM((2, 2 * piece, units), BF16),
        pltpu.VMEM((2, 2 * piece, units), BF16),
        pltpu.VMEM((2, units, 2 * piece), BF16),
        pltpu.VMEM(saved_pre.shape[1:], BF16),
        pltpu.VMEM(saved_out.shape[1:], BF16),
        pltpu.VMEM((2, slots, units), BF16),
        pltpu.VMEM((2, batch, LANES), F32),
        pltpu.VMEM((2, batch, LANES), F32),
        pltpu.VMEM((2, batch, slots), BF16),
        pltpu.VMEM((2, batch, model), BF16),
        pltpu.VMEM((2, batch, units), F32),
        pltpu.VMEM((2, batch, units), F32),
        pltpu.VMEM((2, batch, units), F32),
        pltpu.VMEM((2, batch, units), BF16),
        pltpu.VMEM((2, batch, units), BF16),
        pltpu.VMEM((2, batch, units), BF16),
        pltpu.VMEM((n_dp, 2, bslots, piece), BF16),
        pltpu.VMEM((2, n_chip, 2, 8, piece), BF16),
        pltpu.VMEM((2, n_chip, 2, 8, piece), BF16),
        pltpu.VMEM((2, n_chip, 16, piece), F32),
        pltpu.VMEM((n_chip, 2, 16, piece), BF16),
        pltpu.VMEM((n_chip, 2, 16, piece), BF16),
        pltpu.VMEM((2, 2, 8, piece), BF16),
        dma((6,)),
        dma((3, 2)),
        dma((2,)),
        dma((n_chip, 2)),
        dma((n_chip,)),
        dma((n_chip,)),
        dma((n_dp - 1,)), dma((n_dp - 1,)), dma((n_dp - 1, 2)), dma((n_dp - 1, 2)),
        dma((2, 2)), dma((2, 2)),
        dma((n_chip,)), dma((n_chip,)),
        dma((2, 2)), dma((4,)),
    ]
    parts = pl.pallas_call(
        functools.partial(kernel, n_pipe, n_dev, n_dp, FE // units),
        out_shape=(
            shape((4, 8, piece), BF16),
            shape((n_dp, 2, bslots, piece), BF16),
            shape((n_dp, slots, units), BF16),
            shape((2, acts_fwd.shape[1]), F32),
        ),
        in_specs=[hbm] * 11,
        out_specs=(vmem,) * 4,
        scratch_shapes=scratch,
        compiler_params=pltpu.CompilerParams(
            collective_id=0, has_side_effects=True, vmem_limit_bytes=36 * 1024 * 1024
        ),
        name="relay_layer",
    )(*map(lambda a: pltpu.with_memory_space_constraint(a, pltpu.HBM), (
        acts_fwd[0], cot_bwd[0], ids_fwd[0].T, scores_fwd[0].T, ids_bwd[0].T, scores_bwd[0].T,
        saved_pre[0], saved_out[0],
        w_gate[0].reshape(2, 2 * piece, units), w_up[0].reshape(2, 2 * piece, units), w_down[0],
    )))
    acts_sent, grads_sent, score_grads, down_grad = pl.pallas_call(
        functools.partial(finish, n_pipe),
        out_shape=(
            shape(acts_fwd.shape[1:], BF16),
            shape(acts_fwd.shape[1:], BF16),
            shape((2, acts_fwd.shape[1]), F32),
            shape((piece, units), F32),
        ),
        in_specs=[vmem] * 4,
        out_specs=(vmem,) * 4,
        compiler_params=pltpu.CompilerParams(vmem_limit_bytes=16 * 1024 * 1024),
        name="relay_finish",
    )(*parts)
    return (acts_sent[None], grads_sent[None], score_grads.T[None], down_grad[None])


def solution(mesh):
    token_spec = P("pipe", ("expert", "dp"), None)
    in_specs = (
        token_spec, token_spec, token_spec, token_spec, token_spec, token_spec,
        P("pipe", ("expert", "dp"), None, None),
        P("pipe", "dp", None, "expert"),
        P("pipe", None, "expert"),
        P("pipe", None, "expert"),
        P("pipe", "expert", None),
    )
    out_specs = (token_spec, token_spec, token_spec, P("pipe", "dp", "expert"))
    return jax.shard_map(shards, mesh=mesh, in_specs=in_specs, out_specs=out_specs, check_vma=False)
```

```python
import functools

import jax
import jax.numpy as jnp
from jax import lax
from jax.experimental import pallas as pl
from jax.experimental.pallas import tpu as pltpu
from jax.sharding import PartitionSpec as P

FE = 2048
ROUTE = (
    (0, None), (1, 0), (-1, 0), (3, 0), (-3, 0), (2, 3), (-2, 4), (4, 3), (-4, 4), (6, 3), (-6, 4),
    (5, 9), (-5, 10), (7, 9), (-7, 10), (8, 9),
)
LANES = 128
MESH = pl.DeviceIdType.MESH
BF16, F32 = jnp.bfloat16, jnp.float32


def column(row):
    n = row.shape[1]
    i = lax.broadcasted_iota(jnp.int32, (n, n), 0)
    j = lax.broadcasted_iota(jnp.int32, (n, n), 1)
    return jnp.sum(jnp.where(i == j, jnp.broadcast_to(row, (n, n)), 0.0), axis=1, keepdims=True)


def routing_rows(ids_t, scores_t, with_slots):
    ids = ids_t.astype(F32)
    weights = 2.5 * scores_t / jnp.sum(scores_t, axis=0, keepdims=True)
    tokens = ids.shape[1]
    lane = lax.broadcasted_iota(jnp.int32, (tokens, LANES), 1)
    lane_expert = (lane & 3).astype(F32)
    weight = jnp.zeros((tokens, LANES), F32)
    hit = jnp.zeros((tokens, LANES), F32)
    for k in range(2):
        match = column(ids[k : k + 1]) == lane_expert
        weight = weight + jnp.where(match, column(weights[k : k + 1]), 0.0)
        hit = hit + jnp.where(match, 1.0, 0.0)
    slots = jnp.full((tokens, LANES), -1.0, F32)
    if with_slots:
        running = jnp.zeros((1, LANES), F32)
        before = []
        for t in range(tokens):
            before.append(running)
            running = running + hit[t : t + 1]
        slots = jnp.where(hit > 0.0, jnp.concatenate(before, axis=0), -1.0)
    high = weight.astype(BF16).astype(F32)
    middle = (weight - high).astype(BF16).astype(F32)
    low = weight - high - middle
    return jnp.where(lane < 4, high, jnp.where(lane < 8, middle, jnp.where(lane < 12, low, slots)))


def dot(a, b):
    return jnp.dot(a, b, preferred_element_type=F32)


def dot_nt(a, b):
    return lax.dot_general(a, b, (((1,), (1,)), ((), ())), preferred_element_type=F32)


def dot_tn(a, b):
    return lax.dot_general(a, b, (((0,), (0,)), ((), ())), preferred_element_type=F32)


def kernel(
    n_pipe, n_dev, n_dp, group,
    acts_hbm, cot_hbm, ids_fwd_hbm, scores_fwd_hbm, ids_bwd_hbm, scores_bwd_hbm,
    pre_hbm, saved_hbm, wg_hbm, wu_hbm, wd_hbm,
    fin_recv, sc, hid, sg_out,
    acts_ref, cot_ref, ids_fwd_ref, scores_fwd_ref, ids_bwd_ref, scores_bwd_ref,
    x, wg, wu, wd, pre_in, saved, pre, coef, scale, placer, scaled, gate_acc, up_acc, gh_acc,
    hid_b, gg_b, gu_b, sc_send, sib_send, sib_recv, own, rs_send, rs_recv, fin_send,
    small_sem, w_sem, in_sem, ag_recv, ag_send, ag_sib, hid_s, hid_r, sc_s, sc_r,
    sib_s, sib_r, rs_s, rs_r, fin_s, fin_r,
):
    n_chip = n_dev // 2
    half = n_chip // 2
    pipe = lax.axis_index("pipe")
    me = lax.axis_index("expert")
    mine_dp = lax.axis_index("dp")
    z, core = lax.div(me, 2), lax.rem(me, 2)
    sib = z * 2 + 1 - core
    before, after = lax.rem(pipe + n_pipe - 1, n_pipe), lax.rem(pipe + 1, n_pipe)
    expert = lax.div(me, group)
    tiles = x.shape[2]
    piece = rs_send.shape[3]
    per_piece = piece // LANES
    per_half = 2 * per_piece
    model = 4 * piece
    slots = pre_in.shape[0]
    cap = slots // n_dev
    batch = half * 16
    bslots = half * 2 * cap

    edges = [(c, ROUTE[c][1]) for c in range(1, n_chip)]

    def chip_at(step):
        return lax.rem(z + step + n_chip, n_chip) * 2 + core

    def remote(src, dst, send_sem, recv_sem, **where):
        return pltpu.make_async_remote_copy(
            src_ref=src, dst_ref=dst, send_sem=send_sem, recv_sem=recv_sem,
            device_id=where, device_id_type=MESH,
        )

    small = [
        pltpu.make_async_copy(source, target, small_sem.at[i])
        for i, (source, target) in enumerate((
            (acts_hbm, acts_ref), (cot_hbm, cot_ref), (ids_fwd_hbm, ids_fwd_ref),
            (scores_fwd_hbm, scores_fwd_ref), (ids_bwd_hbm, ids_bwd_ref), (scores_bwd_hbm, scores_bwd_ref),
        ))
    ]
    for copy in small:
        copy.start()
    barrier = pltpu.get_barrier_semaphore()
    peers = [dict(expert=chip_at(step)) for step in sorted(set(ROUTE[c][0] - ROUTE[p][0] for c, p in edges)
             | set(ROUTE[p][0] - ROUTE[c][0] for c, p in edges))]
    peers += [dict(expert=sib)]
    peers += [dict(dp=lax.rem(mine_dp + r, n_dp)) for r in range(1, n_dp)]
    peers += [dict(pipe=p, expert=d) for p in (before, after) for d in (me, sib)]
    for peer in peers:
        pl.semaphore_signal(barrier, inc=1, device_id=peer, device_id_type=MESH)

    side = [pltpu.make_async_copy(pre_hbm, pre_in, in_sem.at[0]), pltpu.make_async_copy(saved_hbm, saved, in_sem.at[1])]
    loads = []
    for q in range(2):
        cols = pl.ds(q * 2 * piece, 2 * piece)
        loads += [
            pltpu.make_async_copy(wg_hbm.at[q], wg.at[q], w_sem.at[0, q]),
            pltpu.make_async_copy(wu_hbm.at[q], wu.at[q], w_sem.at[1, q]),
            pltpu.make_async_copy(wd_hbm.at[:, cols], wd.at[q], w_sem.at[2, q]),
        ]
    for load in side + loads:
        load.start()

    for copy in small:
        copy.wait()
    x[0, 0, 0] = jnp.concatenate(
        [
            routing_rows(ids_fwd_ref[...], scores_fwd_ref[...], False),
            routing_rows(ids_bwd_ref[...], scores_bwd_ref[...], True),
        ],
        axis=0,
    ).astype(BF16)
    for t in range(tiles - 1):
        part = pl.ds(t * LANES, LANES)
        x[0, 0, 1 + t] = jnp.concatenate([acts_ref[:, part].astype(F32), cot_ref[:, part].astype(F32)], axis=0).astype(BF16)

    pl.semaphore_wait(barrier, len(peers))

    def pass_rows(c):
        p = ROUTE[c][1]
        return remote(
            x.at[p, 0], x.at[c, 0], ag_send.at[c], ag_recv.at[c, 0], expert=chip_at(ROUTE[c][0] - ROUTE[p][0])
        )

    def pass_children(p):
        for c, parent in edges:
            if parent == p:
                pass_rows(c).start()

    def sib_rows(p):
        return remote(x.at[p, 0], x.at[p, 1], ag_sib.at[p], ag_recv.at[p, 1], expert=sib)

    for c in (3, 4, 1, 2):
        pass_rows(c).start()
    sib_rows(0).start()

    def take_rows(*places):
        for p in places:
            pass_rows(p).wait_recv()
            pass_children(p)
            sib_rows(p).start()

    def local_inputs():
        for copy in side:
            copy.wait()
        both = pre_in[...].astype(F32)
        gate_pre, up_pre = both[:, 0, :], both[:, 1, :]
        pre[0], pre[1] = gate_pre.astype(BF16), up_pre.astype(BF16)
        rows = (gate_pre * jax.nn.sigmoid(gate_pre) * up_pre).astype(BF16)
        i = lax.broadcasted_iota(jnp.int32, (slots, slots), 0)
        j = lax.broadcasted_iota(jnp.int32, (slots, slots), 1)
        chip, other, slot = lax.div(i, 2 * cap), lax.rem(lax.div(i, cap), 2), lax.rem(i, cap)
        wanted = origin(chip, other) * cap + slot
        swap = jnp.where(j == wanted, 1.0, 0.0).astype(BF16)
        hid[n_dp - 1] = dot(swap, rows).astype(BF16)

    def origin(p, other):
        step = jnp.zeros_like(p)
        for i in range(n_chip):
            step = jnp.where(p == i, ROUTE[i][0], step)
        chip = lax.rem(z - step + n_chip, n_chip)
        return chip * 2 + jnp.where(other == 0, core, 1 - core)

    def hid_copy(r):
        return remote(
            hid.at[n_dp - 1], hid.at[r - 1], hid_s.at[r - 1], hid_r.at[r - 1], dp=lax.rem(mine_dp + r, n_dp)
        )

    def score_gradients():
        scores = scores_bwd_ref[...]
        token = lax.broadcasted_iota(jnp.int32, scores.shape, 1)
        dots = jnp.zeros(scores.shape, F32)
        for t in range(scores.shape[1]):
            product = saved[t].astype(F32) * cot_ref[t : t + 1, :].astype(F32)
            dots = dots + jnp.where(token == t, jnp.sum(product, axis=1, keepdims=True), 0.0)
        total = jnp.sum(scores, axis=0, keepdims=True)
        sg_out[...] = 2.5 / total * (dots - jnp.sum(dots * scores, axis=0, keepdims=True) / total)

    def tile_rows(b, t):
        return x[b * half : (b + 1) * half, :, t].reshape(batch, LANES)

    def half_rows(b, q):
        return jnp.concatenate([tile_rows(b, 1 + q * per_half + t) for t in range(per_half)], axis=1)

    def is_forward(shape):
        return (lax.broadcasted_iota(jnp.int32, shape, 0) & 7) < 4

    def route(b):
        for p in range(b * half, (b + 1) * half):
            sib_rows(p).wait_recv()
        table = tile_rows(b, 0).astype(F32)
        lane = lax.broadcasted_iota(jnp.int32, (batch, LANES), 1)
        mine = (lane < 12) & ((lane & 3) == expert)
        weight = jnp.sum(jnp.where(mine, table, 0.0), axis=1, keepdims=True)
        slot = jnp.sum(jnp.where(lane == expert + 12, table, 0.0), axis=1, keepdims=True)
        coef[b] = jnp.broadcast_to(weight, (batch, LANES))
        scale[b] = jnp.where(is_forward((batch, LANES)), coef[b], 1.0)
        row = lax.broadcasted_iota(jnp.int32, (batch, 1), 0)
        device = origin(b * half + (row >> 4), (row >> 3) & 1)
        target = jnp.where(slot < 0.0, -1.0, slot + (cap * device).astype(F32))
        ids = lax.broadcasted_iota(jnp.int32, (batch, slots), 1).astype(F32)
        placer[b] = jnp.where(ids == target, 1.0, 0.0).astype(BF16)
        weights = coef[b]
        for t in range(tiles - 1):
            scaled[b, :, t * LANES : (t + 1) * LANES] = (weights * tile_rows(b, 1 + t).astype(F32)).astype(BF16)
        near = jnp.where(slot < 0.0, -1.0, slot + (cap * (row >> 3)).astype(F32))
        near_ids = lax.broadcasted_iota(jnp.int32, (batch, bslots), 1).astype(F32)
        near_placer = jnp.where(near_ids == near, 1.0, 0.0).astype(BF16)
        for q in range(4):
            part = scaled[b, :, q * piece : (q + 1) * piece]
            sc_send[q, b] = dot_tn(near_placer, part).astype(BF16)
        for r in range(1, n_dp):
            sc_copy(r, b).start()

    def sc_copy(r, b):
        peer = lax.rem(mine_dp + r, n_dp)
        return remote(sc_send.at[peer, b], sc.at[r - 1, b], sc_s.at[r - 1, b], sc_r.at[r - 1, b], dp=peer)

    def gate_up(b, q):
        rows = half_rows(b, q)
        g, u = dot(rows, wg[q]), dot(rows, wu[q])
        if q == 0:
            gate_acc[b], up_acc[b] = g, u
        else:
            gate_acc[b] += g
            up_acc[b] += u

    def grad_in(b):
        value = None
        for q in range(2):
            term = dot_nt(scaled[b, :, q * 2 * piece : (q + 1) * 2 * piece], wd[q])
            value = term if value is None else value + term
        gh_acc[b] = value

    def activate(b):
        forward = is_forward((batch, 1))
        gate = gate_acc[b]
        hid_b[b] = jnp.where(forward, gate * jax.nn.sigmoid(gate) * up_acc[b], 0.0).astype(BF16)
        gate_pre = dot(placer[b], pre[0])
        up_pre = dot(placer[b], pre[1])
        sg = jax.nn.sigmoid(gate_pre)
        grad_hidden = jnp.where(forward, 0.0, gh_acc[b])
        gg_b[b] = (grad_hidden * up_pre * sg * (1.0 + gate_pre * (1.0 - sg))).astype(BF16)
        gu_b[b] = (grad_hidden * gate_pre * sg).astype(BF16)

    def output(b, q, k):
        part = slice(k * piece, (k + 1) * piece)
        value = dot(hid_b[b], wd[q, :, part]) + dot_nt(gg_b[b], wg[q, part, :]) + dot_nt(gu_b[b], wu[q, part, :])
        return scale[b][:, 0:1] * value

    spans = [pl.ds(0, half), pl.ds(half, 3), pl.ds(half + 3, half - 3)]

    def sib_copy(k, i):
        return remote(
            sib_send.at[k, spans[i]], sib_recv.at[k, spans[i]], sib_s.at[k, i], sib_r.at[k, i], expert=sib
        )

    def output_sib(b, k):
        value = output(b, 1 - core, k).reshape(half, 2, 8, piece).astype(BF16)
        sib_send[k, b * half : (b + 1) * half, 0] = value[:, 1]
        sib_send[k, b * half : (b + 1) * half, 1] = value[:, 0]
        for i in (2, 1) if b == 1 else (0,):
            sib_copy(k, i).start()

    def output_own(b, k):
        own[k, b * half : (b + 1) * half] = output(b, core, k).reshape(half, 16, piece)

    def sib_wait(i):
        for k in range(2):
            sib_copy(k, i).wait_recv()

    def pass_sum(c):
        p = ROUTE[c][1]
        return remote(
            rs_send.at[c], rs_recv.at[c], rs_s.at[c], rs_r.at[c], expert=chip_at(ROUTE[p][0] - ROUTE[c][0])
        )

    def total(p, k):
        value = own[k, p] + sib_recv[k, p].astype(F32).reshape(16, piece)
        for c, parent in edges:
            if parent == p:
                value = value + rs_recv[c, k].astype(F32)
        return value

    def give_sums(*places):
        for p in places:
            for c, parent in edges:
                if parent == p:
                    pass_sum(c).wait_recv()
            for k in range(2):
                rs_send[p, k] = total(p, k).astype(BF16)
            pass_sum(p).start()

    local_inputs()
    for r in range(1, n_dp):
        hid_copy(r).start()
    take_rows(1, 2, 3, 4)
    score_gradients()
    take_rows(5, 6, 7, 8, 9, 10)
    route(0)
    take_rows(11, 12, 13, 14, 15)
    for load in loads:
        load.wait()
    gate_up(0, 0)
    gate_up(0, 1)
    route(1)
    gate_up(1, 0)
    gate_up(1, 1)
    grad_in(1)
    activate(1)
    output_sib(1, 0)
    output_sib(1, 1)
    output_own(1, 0)
    output_own(1, 1)
    sib_wait(2)
    give_sums(15, 13, 14, 11, 12)
    grad_in(0)
    activate(0)
    output_sib(0, 0)
    output_sib(0, 1)
    sib_wait(1)
    give_sums(9, 10)
    output_own(0, 0)
    output_own(0, 1)
    sib_wait(0)
    give_sums(5, 6, 7, 8, 1, 2)
    give_sums(3, 4)
    for c, parent in edges:
        if parent == 0:
            pass_sum(c).wait_recv()
    fin_copies = []
    for k in range(2):
        first = 1 + core * per_half + k * per_piece
        start = jnp.concatenate([x[0, :, first + t].reshape(16, LANES) for t in range(per_piece)], axis=1)
        fin_send[k] = (start.astype(F32) + total(0, k)).astype(BF16).reshape(2, 8, piece)
        for i in range(2):
            q = core * 2 + k
            fin_copies.append(remote(
                fin_send.at[k, i], fin_recv.at[q], fin_s.at[k, i], fin_r.at[q],
                pipe=before, expert=me if i == 0 else sib,
            ))
            fin_copies[-1].start()

    for b in range(2):
        sc[n_dp - 1, b] = sc_send[mine_dp, b]
    for r in range(1, n_dp):
        hid_copy(r).wait()
        for b in range(2):
            sc_copy(r, b).wait()
    for k in range(2):
        for i in range(len(spans)):
            sib_copy(k, i).wait_send()
    for c in range(1, n_chip):
        pass_rows(c).wait_send()
        pass_sum(c).wait_send()
    for p in range(n_chip):
        sib_rows(p).wait_send()
    for copy in fin_copies:
        copy.wait_send()
    for q in range(4):
        remote(fin_send.at[0, 0], fin_recv.at[q], fin_s.at[0, 0], fin_r.at[q], expert=sib).wait_recv()


def finish(n_pipe, fin, sc, hid, sg, acts_out, grads_out, sg_out, down_out):
    last = lax.axis_index("pipe") == n_pipe - 1
    pieces, _, piece = fin.shape
    for q in range(pieces):
        value = jnp.where(last, 0.0, fin[q].astype(F32)).astype(BF16)
        acts_out[:, q * piece : (q + 1) * piece] = value[0:4]
        grads_out[:, q * piece : (q + 1) * piece] = value[4:8]
    sg_out[...] = sg[...]
    rows = hid.shape[0] * hid.shape[1]
    down_out[...] = dot_tn(sc[...].reshape(rows, piece), hid[...].reshape(rows, hid.shape[2]))


def shards(
    acts_fwd, ids_fwd, scores_fwd, cot_bwd, ids_bwd, scores_bwd, saved_out, saved_pre, w_gate, w_up, w_down,
):
    n_pipe, n_dev, n_dp = lax.axis_size("pipe"), lax.axis_size("expert"), lax.axis_size("dp")
    model, units = w_gate.shape[1:]
    slots = saved_pre.shape[1]
    piece = model // 4
    n_chip = n_dev // 2
    half = n_chip // 2
    batch = half * 16
    bslots = slots // 2
    tiles = model // LANES + 1
    vmem = pl.BlockSpec(memory_space=pltpu.VMEM)
    hbm = pl.BlockSpec(memory_space=pltpu.HBM)
    dma = pltpu.SemaphoreType.DMA
    shape = jax.ShapeDtypeStruct
    scratch = [
        pltpu.VMEM(acts_fwd.shape[1:], BF16),
        pltpu.VMEM(acts_fwd.shape[1:], BF16),
        pltpu.VMEM((2, acts_fwd.shape[1]), jnp.int32),
        pltpu.VMEM((2, acts_fwd.shape[1]), F32),
        pltpu.VMEM((2, acts_fwd.shape[1]), jnp.int32),
        pltpu.VMEM((2, acts_fwd.shape[1]), F32),
        pltpu.VMEM((n_chip, 2, tiles, 8, LANES), BF16),
        pltpu.VMEM((2, 2 * piece, units), BF16),
        pltpu.VMEM((2, 2 * piece, units), BF16),
        pltpu.VMEM((2, units, 2 * piece), BF16),
        pltpu.VMEM(saved_pre.shape[1:], BF16),
        pltpu.VMEM(saved_out.shape[1:], BF16),
        pltpu.VMEM((2, slots, units), BF16),
        pltpu.VMEM((2, batch, LANES), F32),
        pltpu.VMEM((2, batch, LANES), F32),
        pltpu.VMEM((2, batch, slots), BF16),
        pltpu.VMEM((2, batch, model), BF16),
        pltpu.VMEM((2, batch, units), F32),
        pltpu.VMEM((2, batch, units), F32),
        pltpu.VMEM((2, batch, units), F32),
        pltpu.VMEM((2, batch, units), BF16),
        pltpu.VMEM((2, batch, units), BF16),
        pltpu.VMEM((2, batch, units), BF16),
        pltpu.VMEM((n_dp, 2, bslots, piece), BF16),
        pltpu.VMEM((2, n_chip, 2, 8, piece), BF16),
        pltpu.VMEM((2, n_chip, 2, 8, piece), BF16),
        pltpu.VMEM((2, n_chip, 16, piece), F32),
        pltpu.VMEM((n_chip, 2, 16, piece), BF16),
        pltpu.VMEM((n_chip, 2, 16, piece), BF16),
        pltpu.VMEM((2, 2, 8, piece), BF16),
        dma((6,)),
        dma((3, 2)),
        dma((2,)),
        dma((n_chip, 2)),
        dma((n_chip,)),
        dma((n_chip,)),
        dma((n_dp - 1,)), dma((n_dp - 1,)), dma((n_dp - 1, 2)), dma((n_dp - 1, 2)),
        dma((2, 3)), dma((2, 3)),
        dma((n_chip,)), dma((n_chip,)),
        dma((2, 2)), dma((4,)),
    ]
    parts = pl.pallas_call(
        functools.partial(kernel, n_pipe, n_dev, n_dp, FE // units),
        out_shape=(
            shape((4, 8, piece), BF16),
            shape((n_dp, 2, bslots, piece), BF16),
            shape((n_dp, slots, units), BF16),
            shape((2, acts_fwd.shape[1]), F32),
        ),
        in_specs=[hbm] * 11,
        out_specs=(vmem,) * 4,
        scratch_shapes=scratch,
        compiler_params=pltpu.CompilerParams(
            collective_id=0, has_side_effects=True, vmem_limit_bytes=36 * 1024 * 1024
        ),
        name="relay_layer",
    )(*map(lambda a: pltpu.with_memory_space_constraint(a, pltpu.HBM), (
        acts_fwd[0], cot_bwd[0], ids_fwd[0].T, scores_fwd[0].T, ids_bwd[0].T, scores_bwd[0].T,
        saved_pre[0], saved_out[0],
        w_gate[0].reshape(2, 2 * piece, units), w_up[0].reshape(2, 2 * piece, units), w_down[0],
    )))
    acts_sent, grads_sent, score_grads, down_grad = pl.pallas_call(
        functools.partial(finish, n_pipe),
        out_shape=(
            shape(acts_fwd.shape[1:], BF16),
            shape(acts_fwd.shape[1:], BF16),
            shape((2, acts_fwd.shape[1]), F32),
            shape((piece, units), F32),
        ),
        in_specs=[vmem] * 4,
        out_specs=(vmem,) * 4,
        compiler_params=pltpu.CompilerParams(vmem_limit_bytes=16 * 1024 * 1024),
        name="relay_finish",
    )(*parts)
    return (acts_sent[None], grads_sent[None], score_grads.T[None], down_grad[None])


def solution(mesh):
    token_spec = P("pipe", ("expert", "dp"), None)
    in_specs = (
        token_spec, token_spec, token_spec, token_spec, token_spec, token_spec,
        P("pipe", ("expert", "dp"), None, None),
        P("pipe", "dp", None, "expert"),
        P("pipe", None, "expert"),
        P("pipe", None, "expert"),
        P("pipe", "expert", None),
    )
    out_specs = (token_spec, token_spec, token_spec, P("pipe", "dp", "expert"))
    return jax.shard_map(shards, mesh=mesh, in_specs=in_specs, out_specs=out_specs, check_vma=False)
```
